32 devices in a mesh: macro: 8 (over y, x, core), rve: 4 (over z).
Axes of the slice: x: 2, y: 2, z: 4, core: 2. Of those that a mesh axis runs over, the one named last changes fastest.
Arguments:
- deform: float32 [9, 512], P(None, 'macro'), may hold values from -6 to 6
- plastic: int32 [512], P('macro'), may hold values 0 or 1
- route: int32 [512], P('macro'), may hold values from 0 to 7, as said below
- stiff: float32 [8, 1536], P('macro', 'rve'), may hold values from 0.1 to 2
- cubic: float32 [8, 1536], P('macro', 'rve'), may hold values from 0.5 to 5
- coupling: float32 [8, 24, 2, 64, 64], P('macro', 'rve'), may hold values from -0.75 to 0.75
- conn: int32 [8, 24, 2], P('macro', 'rve'), may hold values from 0 to 5
- iface: float32 [8, 256, 64], P('macro', 'rve'), may hold values from -0.75 to 0.75
- load_map: float32 [8, 9, 1536], P('macro', None, 'rve'), may hold values from -2 to 2
- average_map: float32 [8, 9, 1536], P('macro', None, 'rve'), may hold values from -0.15625 to 0.15625
Outputs:
- stress: float32 [9, 512], P(None, 'macro')
- micro_field: float32 [8, 1536, 128], P('macro', 'rve')
The draws below stay inside these ranges and needn't reach their ends.
Inputs may be any that keep to these rules, and one draw needn't show every extreme that they name: `route`: among the points of one macro section no group is named more than 16 times, and one group is named exactly 16 times by every section. `conn`: an index among the 6 blocks held with the same block row on one device.
All inputs are finite; a program needn't handle non-finite values. No bound on the sum of `plastic` on one device may be relied on, other than what follows from the above.
Results may differ from the reference program's by a relative error of at most 0.0003.
Values sent between devices are 32-bit elements; how exact they have to be, the bound alone decides.
A program may use at most 64 MiB of HBM per device.

```python
import math
import jax
import jax.numpy as jnp
from jax import lax

POINTS_SEC = 64
BLOCKS_DEV = 6
BLOCK = 64
SLOTS = 2
ITERS = 2
NEWTON = 2
GROUPS = 8
CAPACITY = 16
GROUP_SLOTS = 128
POINTS = 512
DOFS_DEV = 384
RVE_BLOCKS = 24
RVE_DOFS = 1536
N_RVE = 4


def draw_route(key, part):
    chosen = jax.random.randint(jax.random.fold_in(key, 1), (), 0, GROUPS).astype(jnp.int32)
    others = jnp.arange((GROUPS - 1) * CAPACITY, dtype=jnp.int32) // CAPACITY
    others = others + (others >= chosen).astype(jnp.int32)

    def one_section(section):
        section_key = jax.random.fold_in(jax.random.fold_in(key, 2), section)
        shuffled = jax.random.permutation(jax.random.fold_in(section_key, 1), others)
        section_rows = jnp.concatenate([jnp.zeros((CAPACITY,), jnp.int32) + chosen, shuffled[:POINTS_SEC - CAPACITY]])
        return jax.random.permutation(jax.random.fold_in(section_key, 2), section_rows)
    return jax.vmap(one_section)(jnp.arange(GROUPS, dtype=jnp.int32)).reshape(POINTS_SEC * GROUPS)


def set_ends(drawn, stream_key, smallest, top_value):
    dims = drawn.shape
    place = [jax.random.randint(jax.random.fold_in(stream_key, axis), (), 0, dims[axis]) for axis in range(len(dims))]
    drawn = drawn.at[tuple(place)].set(smallest)
    longest = dims.index(max(dims))
    place[longest] = (place[longest] + 1) % dims[longest]
    return drawn.at[tuple(place)].set(top_value)


def shard_levels(stream_key, dims, cuts, least, high):
    level, own = 1.0, jax.random.fold_in(stream_key, 6)
    for dim, parts in cuts:
        draws = jnp.exp(jax.random.uniform(jax.random.fold_in(own, dim), (parts,), jnp.float32, least / len(cuts), high / len(cuts)))
        level = level * jnp.repeat(draws, dims[dim] // parts).reshape([-1 if axis == dim else 1 for axis in range(len(dims))])
    return level


def noise(rng, shape, scale, reach, pieces=(), kind=jnp.bfloat16):
    values = jax.random.normal(rng, shape, jnp.float32) * scale
    if len(pieces) > 0:
        values = shard_levels(rng, shape, pieces, -0.22, 0.18) * values
    return jnp.clip(values, min=-reach, max=reach).astype(kind)


def setup_inputs(seed: int = 0) -> dict:
    key_of = jax.random.split(jax.random.key(seed), 11)
    return {
        "deform": noise(key_of[0], (9, POINTS), 1.0, 6.0, ((1, 8),), jnp.float32),
        "plastic": set_ends((jax.random.randint(key_of[1], (POINTS,), 0, 2) < 1).astype(jnp.int32), jax.random.fold_in(key_of[1], 1), 0, 1),
        "route": draw_route(jax.random.fold_in(key_of[10], 71), 0),
        "stiff": jnp.clip(jnp.exp(math.log(2.0) - 2.9957323 * jax.random.uniform(key_of[3], (GROUPS, RVE_DOFS), jnp.float32) ** shard_levels(key_of[3], (GROUPS, RVE_DOFS), ((0, 8), (1, 4)), -0.2, 0.2)), 0.1, 2.0),
        "cubic": jnp.clip(jnp.exp(math.log(5.0) - 2.3025851 * jax.random.uniform(key_of[4], (GROUPS, RVE_DOFS), jnp.float32) ** shard_levels(key_of[4], (GROUPS, RVE_DOFS), ((0, 8), (1, 4)), -0.2, 0.2)), 0.5, 5.0),
        "coupling": noise(key_of[5], (GROUPS, RVE_BLOCKS, SLOTS, BLOCK, BLOCK), BLOCK ** -0.5, 0.75, ((0, 8), (1, 4)), jnp.float32),
        "conn": set_ends(jax.random.randint(key_of[6], (GROUPS, RVE_BLOCKS, SLOTS), 0, BLOCKS_DEV), jax.random.fold_in(key_of[6], 1), 0, BLOCKS_DEV - 1).astype(jnp.int32),
        "iface": noise(key_of[7], (GROUPS, N_RVE * BLOCK, BLOCK), BLOCK ** -0.5, 0.75, ((0, 8), (1, 4)), jnp.float32),
        "load_map": noise(key_of[8], (GROUPS, 9, RVE_DOFS), 9 ** -0.5, 2.0, ((0, 8), (2, 4)), jnp.float32),
        "average_map": noise(key_of[9], (GROUPS, 9, RVE_DOFS), RVE_DOFS ** -0.5, 0.15625, ((0, 8), (2, 4)), jnp.float32),
    }


HIGHEST_PREC = lax.Precision.HIGHEST
EPSILON = 1e-6


def slot_index(route_rows, capacity):
    point_count = route_rows.shape[0]
    position = jnp.arange(point_count, dtype=jnp.int32)
    same_group = route_rows[:, None] == route_rows[None, :]
    before = position[None, :] < position[:, None]
    rank_in = jnp.sum(jnp.where(jnp.logical_and(same_group, before), 1, 0).astype(jnp.int32), axis=1)
    return route_rows * capacity + rank_in


def local_matrix(coupling, conn, stiff):
    blocks, slot_count, block_size, _ = coupling.shape
    spring = jnp.einsum("bsxk,bsyk->bsxy", coupling, coupling, precision=HIGHEST_PREC)
    block_ids = jnp.arange(blocks, dtype=jnp.int32)
    own_mark = (block_ids[None, None, :] == block_ids[:, None, None]).astype(jnp.float32)
    far_mark = jnp.logical_and(block_ids[None, None, :] == conn[:, :, None], conn[:, :, None] != block_ids[:, None, None]).astype(jnp.float32)
    weight = own_mark - far_mark
    pair_mark = jnp.einsum("bsk,bsl->bskl", weight, weight, precision=HIGHEST_PREC)
    assembled = jnp.einsum("bskl,bsxy->kxly", pair_mark, spring, precision=HIGHEST_PREC)
    assembled = assembled.reshape(blocks * block_size, blocks * block_size)
    return assembled + jnp.diag(stiff)


def solve_group(items):
    strain, flag_row, stiff, cubic, coupling, conn, iface, load_map, average_map = items
    part_count = N_RVE
    local_parts = jax.vmap(local_matrix)(coupling.reshape(part_count, BLOCKS_DEV, SLOTS, BLOCK, BLOCK), conn.reshape(part_count, BLOCKS_DEV, SLOTS), stiff.reshape(part_count, DOFS_DEV))
    edge_blocks = iface.reshape(part_count, BLOCK, BLOCK)
    springs = jnp.einsum("qxk,qyk->qxy", edge_blocks, edge_blocks, precision=HIGHEST_PREC)
    next_springs = jnp.roll(springs, -1, axis=0)
    load_cols = jnp.einsum("ci,cp->ip", load_map, strain, precision=HIGHEST_PREC).reshape(part_count, DOFS_DEV, GROUP_SLOTS)
    hard = flag_row[None, None, :] * cubic.reshape(part_count, DOFS_DEV, 1)

    def operate(field):
        product = jnp.einsum("qij,qjp->qip", local_parts, field, precision=HIGHEST_PREC)
        first_rows = field[:, :BLOCK]
        last_rows = field[:, -BLOCK:]
        prev_last = jnp.roll(last_rows, 1, axis=0)
        next_first = jnp.roll(first_rows, -1, axis=0)
        top_flux = jnp.einsum("qij,qjp->qip", springs, first_rows - prev_last, precision=HIGHEST_PREC)
        bottom = jnp.einsum("qij,qjp->qip", next_springs, last_rows - next_first, precision=HIGHEST_PREC)
        product = product.at[:, :BLOCK].add(top_flux)
        product = product.at[:, -BLOCK:].add(bottom)
        return product

    def col_sum(values):
        return jnp.sum(values, axis=(0, 1))

    solution = jnp.zeros_like(load_cols)
    for newton_step in range(NEWTON):
        tangent_add = 3.0 * hard * solution * solution
        right_side = load_cols - operate(solution) - hard * (solution * solution * solution)

        def sweep(turn_index, carried):
            iterate, residue, direct, norm_now = carried
            product = operate(direct) + tangent_add * direct
            step_len = norm_now / (col_sum(direct * product) + EPSILON)
            iterate = iterate + step_len * direct
            residue = residue - step_len * product
            norm_next = col_sum(residue * residue)
            direct = residue + (norm_next / (norm_now + EPSILON)) * direct
            return iterate, residue, direct, norm_next

        start = (jnp.zeros_like(right_side), right_side, right_side, col_sum(right_side * right_side))
        iterate, residue, direct, norm_now = lax.fori_loop(0, ITERS, sweep, start)
        solution = solution + iterate
    field_flat = solution.reshape(RVE_DOFS, GROUP_SLOTS)
    group_stress = jnp.einsum("ci,ip->cp", average_map, field_flat, precision=HIGHEST_PREC)
    return group_stress, field_flat


def partial_slot(route_rows):
    return slot_index(route_rows, CAPACITY)


def reference(deform, plastic, route, stiff, cubic, coupling, conn, iface, load_map, average_map):
    sections = GROUPS
    route_sec = route.reshape(sections, POINTS_SEC)
    slot_ids = jax.vmap(partial_slot)(route_sec)
    places = jnp.arange(GROUPS * CAPACITY, dtype=jnp.int32)
    select = (slot_ids[:, :, None] == places[None, None, :]).astype(jnp.float32)
    deform_sec = deform.reshape(9, sections, POINTS_SEC)
    sent = jnp.einsum("cmi,mis->cms", deform_sec, select, precision=HIGHEST_PREC).reshape(9, sections, GROUPS, CAPACITY)
    received = jnp.transpose(sent, (2, 0, 1, 3)).reshape(GROUPS, 9, GROUP_SLOTS)
    flag_sec = plastic.reshape(sections, POINTS_SEC).astype(jnp.float32)
    flag_sent = jnp.einsum("mi,mis->ms", flag_sec, select, precision=HIGHEST_PREC).reshape(sections, GROUPS, CAPACITY)
    received_flag = jnp.transpose(flag_sent, (1, 0, 2)).reshape(GROUPS, GROUP_SLOTS)
    group_stress, micro_field = lax.map(solve_group, (received, received_flag, stiff, cubic, coupling, conn, iface, load_map, average_map))
    stress_cols = jnp.transpose(group_stress, (1, 0, 2)).reshape(9, GROUPS, sections, CAPACITY)
    stress_sec = jnp.transpose(stress_cols, (0, 2, 1, 3)).reshape(9, sections, GROUPS * CAPACITY)
    stress = jnp.einsum("cms,mis->cmi", stress_sec, select, precision=HIGHEST_PREC).reshape(9, POINTS)
    return stress, micro_field
```

```python
import functools

import jax
import jax.numpy as jnp
from jax import lax
from jax.experimental import pallas as pl
from jax.experimental.pallas import tpu as pltpu
from jax.sharding import PartitionSpec as P

EPSILON = 1e-06
MESH = pl.DeviceIdType.MESH
HIGHEST = lax.Precision.HIGHEST
F32 = jnp.float32
BF16 = jnp.bfloat16
LANES = 128
NT = (((1,), (1,)), ((), ()))


def split(values):
    high = values.astype(BF16)
    return high, (values - high.astype(F32)).astype(BF16)


def dot(left, right):
    return jnp.dot(left, right, preferred_element_type=F32)


def dot_nt(left, right, precision=None):
    return lax.dot_general(left, right, NT, precision=precision, preferred_element_type=F32)


def apply_split(high, low, values):
    value_high, value_low = split(values)
    width = values.shape[1]
    wide = dot(high, jnp.concatenate([value_high, value_low], axis=1))
    return wide[:, :width] + wide[:, width:] + dot(low, value_high)


def square_nt(values):
    high, low = split(values)
    return dot_nt(high, high) + (dot_nt(high, low) + dot_nt(low, high))


def iota(shape, dim):
    return lax.broadcasted_iota(jnp.int32, shape, dim)


def pad_rows(values, rows):
    missing = rows - values.shape[0]
    if missing == 0:
        return values
    return jnp.concatenate([values, jnp.zeros((missing, values.shape[1]), values.dtype)], axis=0)


def col_sum(values):
    return jnp.sum(values, axis=0, keepdims=True)


def kernel(
    groups, parts, capacity,
    deform_ref, plastic_ref, route_ref, stiff_ref, cubic_ref, coupling_ref, conn_ref,
    iface_ref, load_ref, average_ref,
    stress_ref, field_ref,
    factor_high, factor_low, stiff_high, stiff_low,
    out_points, in_points, edge_out, edge_in,
    halo_out, halo_in, sum_buf, part_buf, out_rows, in_rows,
    point_send, point_recv, edge_send, edge_recv, halo_send, halo_recv,
    sum_send, sum_recv, part_send, part_recv, row_send, row_recv,
):
    group = lax.axis_index("macro")
    part = lax.axis_index("rve")
    blocks, slots, block = coupling_ref.shape[1], coupling_ref.shape[2], coupling_ref.shape[3]
    dofs = blocks * block
    points = deform_ref.shape[1]
    comps = deform_ref.shape[0]
    padded = out_points.shape[1]
    columns = groups * capacity
    places = groups * padded

    barrier = pltpu.get_barrier_semaphore()
    for step in range(1, groups):
        pl.semaphore_signal(
            barrier, inc=1, device_id={"macro": lax.rem(group + step, groups)}, device_id_type=MESH
        )
    for step in range(1, parts):
        pl.semaphore_signal(
            barrier, inc=1, device_id={"rve": lax.rem(part + step, parts)}, device_id_type=MESH
        )

    route = route_ref[...]
    hot = (iota((groups, points), 0) == route).astype(F32)
    before = (iota((points, points), 0) < iota((points, points), 1)).astype(BF16)
    rank = col_sum(hot * dot(hot.astype(BF16), before))
    slot = (route * padded).astype(F32) + rank
    select = (iota((places, points), 0).astype(F32) == slot).astype(F32)
    sent = jnp.concatenate(
        [deform_ref[...], plastic_ref[...].astype(F32)], axis=0
    )
    sent = pad_rows(sent, LANES)
    outgoing = dot_nt(select, sent, HIGHEST)
    out_points[...] = outgoing.reshape(groups, padded, LANES)

    maps = pad_rows(jnp.concatenate([load_ref[0], cubic_ref[...]], axis=0), 16)
    edge_out[0:16, :] = jnp.concatenate([maps[:, :block], maps[:, dofs - block:]], axis=1)
    own_edge = iface_ref[0]
    edge_out[16:, :] = jnp.concatenate([own_edge, jnp.zeros((block, LANES - block), F32)], axis=1)

    pl.semaphore_wait(barrier, groups + parts - 2)

    def exchange(source, target, send, recv):
        copies = []
        for step in range(1, groups):
            peer = lax.rem(group + step, groups)
            copies.append(pltpu.make_async_remote_copy(
                src_ref=source.at[peer], dst_ref=target.at[group],
                send_sem=send.at[step - 1], recv_sem=recv.at[step - 1],
                device_id={"macro": peer}, device_id_type=MESH,
            ))
            copies[-1].start()
        return copies

    def share(buffer, send, recv):
        copies = []
        for step in range(1, parts):
            copies.append(pltpu.make_async_remote_copy(
                src_ref=buffer.at[part], dst_ref=buffer.at[part],
                send_sem=send.at[step - 1], recv_sem=recv.at[step - 1],
                device_id={"rve": lax.rem(part + step, parts)}, device_id_type=MESH,
            ))
            copies[-1].start()
        return copies

    after, behind = lax.rem(part + 1, parts), lax.rem(part + parts - 1, parts)

    def to_neighbours(first, last, target, send, recv):
        copies = []
        for place, (source, peer) in enumerate(((last, after), (first, behind))):
            copies.append(pltpu.make_async_remote_copy(
                src_ref=source, dst_ref=target.at[place],
                send_sem=send.at[place], recv_sem=recv.at[place],
                device_id={"rve": peer}, device_id_type=MESH,
            ))
            copies[-1].start()
        return copies

    def arrive(copies):
        for copy in copies:
            copy.wait_recv()

    sends = []
    point_copies = exchange(out_points, in_points, point_send, point_recv)
    edge_copies = to_neighbours(edge_out, edge_out, edge_in, edge_send, edge_recv)
    sends += point_copies + edge_copies
    in_points[group] = out_points[group]

    lane = iota((block, LANES), 1)
    for row in range(blocks):
        pair = jnp.concatenate([coupling_ref[0, row, 0], coupling_ref[0, row, 1]], axis=1)
        high, low = split(pair)
        for near in range(blocks):
            rows = slice(near * block, (near + 1) * block)
            cols = slice(row * LANES, (row + 1) * LANES)
            if near == row:
                factor_high[rows, cols] = high
                factor_low[rows, cols] = low
            else:
                first = jnp.where(conn_ref[0, row, 0] == near, -1.0, 0.0).astype(F32)
                second = jnp.where(conn_ref[0, row, 1] == near, -1.0, 0.0).astype(F32)
                mark = jnp.where(lane < block, first, second).astype(BF16)
                factor_high[rows, cols] = high * mark
                factor_low[rows, cols] = low * mark
    fh, fl = factor_high[...], factor_low[...]
    stiffness = dot_nt(fh, fh) + (dot_nt(fh, fl) + dot_nt(fl, fh))
    diagonal = iota((dofs, dofs), 0) == iota((dofs, dofs), 1)
    stiffness = stiffness + jnp.where(diagonal, stiff_ref[...], 0.0)
    own_spring = square_nt(own_edge)
    own_high, own_low = split(own_spring)
    maps_cols = jnp.transpose(maps)
    average = pad_rows(average_ref[0], 16)
    average_high, average_low = split(average)

    arrive(edge_copies)
    next_spring = square_nt(edge_in[1, 16:, :][:, :block])
    next_high, next_low = split(next_spring)
    high, low = split(stiffness)
    stiff_high[...] = high
    stiff_low[...] = low
    high, low = split(stiffness[:block, :block] + own_spring)
    stiff_high[:block, :block] = high
    stiff_low[:block, :block] = low
    high, low = split(stiffness[dofs - block:, dofs - block:] + next_spring)
    stiff_high[dofs - block:, dofs - block:] = high
    stiff_low[dofs - block:, dofs - block:] = low
    prev_maps = jnp.transpose(edge_in[0, 0:16, :])[block:]
    next_maps = jnp.transpose(edge_in[1, 0:16, :])[:block]
    ghost_maps = jnp.concatenate([prev_maps, next_maps], axis=0)

    arrive(point_copies)

    def compact(rows):
        rows = rows.reshape(places, LANES)
        if padded == capacity:
            return rows
        row, col = iota((columns, places), 0), iota((columns, places), 1)
        take = (col == (row // capacity) * padded + row % capacity).astype(F32)
        return jnp.dot(take, rows, precision=HIGHEST, preferred_element_type=F32)

    strain = jnp.transpose(compact(in_points[...]))[:16]
    flag = strain[comps:comps + 1]
    strain_only = jnp.where(iota((16, columns), 0) < comps, strain, 0.0)
    load = jnp.dot(maps_cols, strain_only, precision=HIGHEST, preferred_element_type=F32)
    ghost_load = jnp.dot(ghost_maps, strain_only, precision=HIGHEST, preferred_element_type=F32)
    hard = maps_cols[:, comps:comps + 1] * flag
    ghost_hard = ghost_maps[:, comps:comps + 1] * flag

    def local(values):
        return apply_split(stiff_high[...], stiff_low[...], values)

    def coupled(product, ghost):
        top = product[:block] - apply_split(own_high, own_low, ghost[:block])
        bottom = product[dofs - block:] - apply_split(next_high, next_low, ghost[block:])
        return jnp.concatenate([top, product[block:dofs - block], bottom], axis=0)

    def start_sum(turn, values):
        sum_buf[turn, part] = pad_rows(jnp.concatenate(values, axis=0), 8)
        return share(sum_buf.at[turn], sum_send.at[turn], sum_recv.at[turn])

    def end_sum(turn, copies):
        arrive(copies)
        total = sum_buf[turn, 0]
        for other in range(1, parts):
            total = total + sum_buf[turn, other]
        return total

    def start_halo(turn, values):
        halo_out[turn, 0] = values[:block]
        halo_out[turn, 1] = values[dofs - block:]
        return to_neighbours(
            halo_out.at[turn, 0], halo_out.at[turn, 1], halo_in.at[turn],
            halo_send.at[turn], halo_recv.at[turn],
        )

    def end_halo(turn, copies):
        arrive(copies)
        return halo_in[turn].reshape(2 * block, columns)

    residue, ghost = load, ghost_load
    solved = None
    turn = 0
    for newton in range(2):
        image = coupled(local(residue), ghost)
        if newton == 1:
            image = image + tangent * residue
        halo_copies = start_halo(turn, image)
        sum_copies = start_sum(2 * newton, [col_sum(residue * residue), col_sum(residue * image)])
        sends += halo_copies + sum_copies
        second = local(image)
        ghost_image = end_halo(turn, halo_copies)
        turn += 1
        second = coupled(second, ghost_image)
        if newton == 1:
            second = second + tangent * image
        else:
            second_copies = start_halo(turn, second)
            sends += second_copies
        sums = end_sum(2 * newton, sum_copies)
        norm, curve = sums[0:1], sums[1:2]
        step_len = norm / (curve + EPSILON)
        left = residue - step_len * image
        left_image = image - step_len * second
        sum_copies = start_sum(
            2 * newton + 1,
            [col_sum(left * left), col_sum(left * left_image), col_sum(left * image)],
        )
        sends += sum_copies
        sums = end_sum(2 * newton + 1, sum_copies)
        left_norm, left_curve, cross = sums[0:1], sums[1:2], sums[2:3]
        ratio = left_norm / (norm + EPSILON)
        next_curve = left_curve + ratio * (2.0 * cross + ratio * curve)
        next_len = left_norm / (next_curve + EPSILON)
        from_start = step_len + next_len * ratio
        change = from_start * residue + next_len * left
        if newton == 0:
            solved = change
            hard_square = hard * solved * solved
            tangent = 3.0 * hard_square
            new_residue = load - (from_start * image + next_len * left_image) - hard_square * solved
            ghost_second = end_halo(turn, second_copies)
            turn += 1
            ghost_left = ghost - step_len * ghost_image
            ghost_left_image = ghost_image - step_len * ghost_second
            ghost_solved = from_start * ghost + next_len * ghost_left
            ghost = (
                ghost_load - (from_start * ghost_image + next_len * ghost_left_image)
                - ghost_hard * ghost_solved * ghost_solved * ghost_solved
            )
            residue = new_residue
        else:
            solved = solved + change

    part_buf[part] = apply_split(average_high, average_low, solved)
    part_copies = share(part_buf, part_send, part_recv)
    field_ref[0] = solved
    arrive(part_copies)
    total = part_buf[0]
    for other in range(1, parts):
        total = total + part_buf[other]
    rows = jnp.transpose(pad_rows(total, LANES))
    if padded != capacity:
        row, col = iota((places, columns), 0), iota((places, columns), 1)
        spread = jnp.logical_and(
            col == (row // padded) * capacity + row % padded, row % padded < capacity
        ).astype(F32)
        rows = jnp.dot(spread, rows, precision=HIGHEST, preferred_element_type=F32)
    out_rows[...] = rows.reshape(groups, padded, LANES)
    row_copies = exchange(out_rows, in_rows, row_send, row_recv)
    sends += part_copies + row_copies
    in_rows[group] = out_rows[group]
    arrive(row_copies)
    back = jnp.transpose(in_rows[...].reshape(places, LANES))[:16]
    picked = jnp.dot(back, select, precision=HIGHEST, preferred_element_type=F32)
    stress_ref[...] = picked[:comps]
    for copy in sends:
        copy.wait_send()


def solution(mesh):
    groups, parts = mesh.shape["macro"], mesh.shape["rve"]

    def shards(deform, plastic, route, stiff, cubic, coupling, conn, iface, load_map, average_map):
        comps, points = deform.shape
        blocks, block = coupling.shape[1], coupling.shape[3]
        dofs = blocks * block
        capacity = 2 * points // groups
        columns = groups * capacity
        padded = -(-capacity // 8) * 8
        vmem = pl.BlockSpec(memory_space=pltpu.VMEM)
        dma = pltpu.SemaphoreType.DMA
        return pl.pallas_call(
            functools.partial(kernel, groups, parts, capacity),
            out_shape=(
                jax.ShapeDtypeStruct((comps, points), F32),
                jax.ShapeDtypeStruct((1, dofs, columns), F32),
            ),
            in_specs=[vmem] * 6 + [pl.BlockSpec(memory_space=pltpu.SMEM)] + [vmem] * 3,
            out_specs=(vmem, vmem),
            scratch_shapes=[
                pltpu.VMEM((dofs, blocks * LANES), BF16),
                pltpu.VMEM((dofs, blocks * LANES), BF16),
                pltpu.VMEM((dofs, dofs), BF16),
                pltpu.VMEM((dofs, dofs), BF16),
                pltpu.VMEM((groups, padded, LANES), F32),
                pltpu.VMEM((groups, padded, LANES), F32),
                pltpu.VMEM((16 + block, LANES), F32),
                pltpu.VMEM((2, 16 + block, LANES), F32),
                pltpu.VMEM((3, 2, block, columns), F32),
                pltpu.VMEM((3, 2, block, columns), F32),
                pltpu.VMEM((4, parts, 8, columns), F32),
                pltpu.VMEM((parts, 16, columns), F32),
                pltpu.VMEM((groups, padded, LANES), F32),
                pltpu.VMEM((groups, padded, LANES), F32),
                dma((groups - 1,)), dma((groups - 1,)),
                dma((2,)), dma((2,)),
                dma((3, 2)), dma((3, 2)),
                dma((4, parts - 1)), dma((4, parts - 1)),
                dma((parts - 1,)), dma((parts - 1,)),
                dma((groups - 1,)), dma((groups - 1,)),
            ],
            compiler_params=pltpu.CompilerParams(
                collective_id=0, has_side_effects=True, vmem_limit_bytes=32 * 1024 * 1024
            ),
        )(
            deform, plastic[None], route[None], stiff, cubic, coupling, conn,
            iface, load_map, average_map,
        )

    return jax.shard_map(
        shards,
        mesh=mesh,
        in_specs=(
            P(None, "macro"),
            P("macro"),
            P("macro"),
            P("macro", "rve"),
            P("macro", "rve"),
            P("macro", "rve", None, None, None),
            P("macro", "rve", None),
            P("macro", "rve", None),
            P("macro", None, "rve"),
            P("macro", None, "rve"),
        ),
        out_specs=(P(None, "macro"), P("macro", "rve", None)),
        check_vma=False,
    )
```

```python
import functools

import jax
import jax.numpy as jnp
from jax import lax
from jax.experimental import pallas as pl
from jax.experimental.pallas import tpu as pltpu
from jax.sharding import PartitionSpec as P

EPSILON = 1e-06
MESH = pl.DeviceIdType.MESH
HIGHEST = lax.Precision.HIGHEST
F32 = jnp.float32
BF16 = jnp.bfloat16
LANES = 128
NT = (((1,), (1,)), ((), ()))


def split(values):
    high = values.astype(BF16)
    return high, (values - high.astype(F32)).astype(BF16)


def dot(left, right):
    return jnp.dot(left, right, preferred_element_type=F32)


def dot_nt(left, right, precision=None):
    return lax.dot_general(left, right, NT, precision=precision, preferred_element_type=F32)


def apply_split(high, low, values):
    value_high, value_low = split(values)
    width = values.shape[1]
    wide = dot(high, jnp.concatenate([value_high, value_low], axis=1))
    return wide[:, :width] + wide[:, width:] + dot(low, value_high)


def apply_rows(values, high, low):
    value_high, value_low = split(values)
    rows = values.shape[0]
    tall = dot(jnp.concatenate([value_high, value_low], axis=0), high)
    return tall[:rows] + tall[rows:] + dot(value_high, low)


def square_nt(values):
    high, low = split(values)
    return dot_nt(high, high) + (dot_nt(high, low) + dot_nt(low, high))


def iota(shape, dim):
    return lax.broadcasted_iota(jnp.int32, shape, dim)


def pad_rows(values, rows):
    missing = rows - values.shape[0]
    if missing == 0:
        return values
    return jnp.concatenate([values, jnp.zeros((missing, values.shape[1]), values.dtype)], axis=0)


def col_sum(values):
    return jnp.sum(values, axis=0, keepdims=True)


def kernel(
    groups, parts, capacity,
    deform_hbm, plastic_hbm, route_hbm, stiff_hbm, cubic_hbm, coupling_hbm, conn_ref,
    iface_hbm, load_hbm, average_hbm,
    stress_ref, field_ref,
    deform_ref, plastic_ref, route_ref, stiff_ref, cubic_ref, coupling_ref,
    iface_ref, load_ref, average_ref,
    whole, stiff_high, stiff_low,
    out_points, in_points, edge_out, edge_in,
    halo_out, halo_in, gram_buf, first_buf, second_buf, out_rows, in_rows,
    input_sem,
    point_send, point_recv, edge_send, edge_recv, halo_send, halo_recv,
    gram_send, gram_recv, first_send, first_recv, second_send, second_recv, row_send, row_recv,
):
    group = lax.axis_index("macro")
    part = lax.axis_index("rve")
    blocks, slots, block = coupling_ref.shape[1], coupling_ref.shape[2], coupling_ref.shape[3]
    dofs = blocks * block
    comps, points = deform_ref.shape
    padded = out_points.shape[1]
    columns = groups * capacity
    places = groups * padded

    barrier = pltpu.get_barrier_semaphore()
    for step in range(1, parts):
        pl.semaphore_signal(
            barrier, inc=1, device_id={"rve": lax.rem(part + step, parts)}, device_id_type=MESH
        )
    for step in range(1, groups):
        pl.semaphore_signal(
            barrier, inc=1, device_id={"macro": lax.rem(group + step, groups)}, device_id_type=MESH
        )

    loads = []
    for source, target in (
        (coupling_hbm, coupling_ref), (iface_hbm, iface_ref), (load_hbm, load_ref),
        (cubic_hbm, cubic_ref), (stiff_hbm, stiff_ref), (deform_hbm, deform_ref),
        (plastic_hbm, plastic_ref), (route_hbm, route_ref), (average_hbm, average_ref),
    ):
        loads.append(pltpu.make_async_copy(source, target, input_sem.at[len(loads)]))
        loads[-1].start()
    for copy in loads:
        copy.wait()

    def exchange(source, target, send, recv):
        copies = []
        for step in range(1, groups):
            peer = lax.rem(group + step, groups)
            copies.append(pltpu.make_async_remote_copy(
                src_ref=source.at[peer], dst_ref=target.at[group],
                send_sem=send.at[step - 1], recv_sem=recv.at[step - 1],
                device_id={"macro": peer}, device_id_type=MESH,
            ))
            copies[-1].start()
        return copies

    def share(buffer, send, recv):
        copies = []
        for step in range(1, parts):
            copies.append(pltpu.make_async_remote_copy(
                src_ref=buffer.at[part], dst_ref=buffer.at[part],
                send_sem=send.at[step - 1], recv_sem=recv.at[step - 1],
                device_id={"rve": lax.rem(part + step, parts)}, device_id_type=MESH,
            ))
            copies[-1].start()
        return copies

    after, behind = lax.rem(part + 1, parts), lax.rem(part + parts - 1, parts)

    def to_neighbours(first, last, target, send, recv):
        copies = []
        for place, (source, peer) in enumerate(((last, after), (first, behind))):
            copies.append(pltpu.make_async_remote_copy(
                src_ref=source, dst_ref=target.at[place],
                send_sem=send.at[place], recv_sem=recv.at[place],
                device_id={"rve": peer}, device_id_type=MESH,
            ))
            copies[-1].start()
        return copies

    def arrive(copies):
        for copy in copies:
            copy.wait_recv()

    def gathered(buffer):
        total = buffer[0]
        for other in range(1, parts):
            total = total + buffer[other]
        return total

    lane = iota((block, LANES), 1) < block
    doubled = []
    for row in range(blocks):
        square = square_nt(coupling_ref[0, row].reshape(slots * block, block))
        doubled.append([])
        for slot in range(slots):
            spring = square[slot * block:(slot + 1) * block, slot * block:(slot + 1) * block]
            doubled[row].append(jnp.concatenate([spring, spring], axis=1))

    def mark(row, slot, far):
        if row == far:
            return jnp.float32(0.0)
        return jnp.where(conn_ref[0, slot, row] == far, 1.0, 0.0).astype(F32)

    for row in range(blocks):
        own = doubled[row][0]
        for slot in range(1, slots):
            own = own + doubled[row][slot]
        for other in range(blocks):
            if other != row:
                for slot in range(slots):
                    own = own + doubled[other][slot] * mark(other, slot, row)
        for pair in range(blocks // 2):
            left, right = 2 * pair, 2 * pair + 1
            value = jnp.zeros((block, LANES), F32)
            for slot in range(slots):
                value = value - doubled[row][slot] * jnp.where(
                    lane, mark(row, slot, left), mark(row, slot, right)
                )
                value = value - jnp.where(
                    lane, doubled[left][slot] * mark(left, slot, row),
                    doubled[right][slot] * mark(right, slot, row),
                )
            if row == left:
                value = value + jnp.where(lane, own, 0.0)
            if row == right:
                value = value + jnp.where(lane, 0.0, own)
            whole[row * block:(row + 1) * block, pair * LANES:(pair + 1) * LANES] = value

    own_edge = iface_ref[0]
    own_spring = square_nt(own_edge)
    own_high, own_low = split(own_spring)
    diagonal = iota((dofs, dofs), 0) == iota((dofs, dofs), 1)
    stiffness = whole[...] + jnp.where(diagonal, stiff_ref[...], 0.0)
    high, low = split(stiffness)
    stiff_high[...] = high
    stiff_low[...] = low
    high, low = split(stiffness[:block, :block] + own_spring)
    stiff_high[:block, :block] = high
    stiff_low[:block, :block] = low

    maps = pad_rows(load_ref[:, 0, :], 16)
    cubic = pad_rows(cubic_ref[...], 16)

    def ends(values):
        return jnp.concatenate([values[:, :block], values[:, dofs - block:]], axis=1)

    image_map = apply_rows(maps, stiff_high[...], stiff_low[...])
    edge_out[0:16, :] = ends(maps)
    edge_out[16:32, :] = ends(image_map)
    edge_out[32:48, :] = ends(cubic)
    edge_out[48:, :] = jnp.concatenate([own_edge[:block // 2], own_edge[block // 2:]], axis=1)

    pl.semaphore_wait(barrier, groups + parts - 2)

    sends = []
    edge_copies = to_neighbours(edge_out, edge_out, edge_in, edge_send, edge_recv)

    route = route_ref[...]
    hot = (iota((groups, points), 0) == route).astype(F32)
    before = (iota((points, points), 0) < iota((points, points), 1)).astype(BF16)
    rank = col_sum(hot * dot(hot.astype(BF16), before))
    slot_of = (route * padded).astype(F32) + rank
    select = (iota((places, points), 0).astype(F32) == slot_of).astype(F32)
    sent = pad_rows(
        jnp.concatenate([deform_ref[...], plastic_ref[...].astype(F32)], axis=0), LANES
    )
    outgoing = dot_nt(select, sent, HIGHEST)
    out_points[...] = outgoing.reshape(groups, padded, LANES)
    point_copies = exchange(out_points, in_points, point_send, point_recv)
    sends += point_copies + edge_copies
    in_points[group] = out_points[group]
    average_high, average_low = split(pad_rows(average_ref[:, 0, :], 16))

    arrive(edge_copies)
    packed = edge_in[1, 48:, :]
    next_spring = square_nt(jnp.concatenate([packed[:, :block], packed[:, block:]], axis=0))
    next_high, next_low = split(next_spring)
    high, low = split(stiffness[dofs - block:, dofs - block:] + next_spring)
    stiff_high[dofs - block:, dofs - block:] = high
    stiff_low[dofs - block:, dofs - block:] = low

    def own_rows(values):
        return apply_rows(values, own_high, own_low)

    def next_rows(values):
        return apply_rows(values, next_high, next_low)

    prev_edge, next_edge = edge_in[0], edge_in[1]
    prev_map, next_map = prev_edge[0:16, block:], next_edge[0:16, :block]
    first_map, last_map = maps[:, :block], maps[:, dofs - block:]
    through_own = own_rows(jnp.concatenate([prev_map, first_map], axis=0))
    through_next = next_rows(jnp.concatenate([next_map, last_map], axis=0))
    prev_image = prev_edge[16:32, block:] + through_own[:16] - through_own[16:]
    next_image = next_edge[16:32, :block] - through_next[16:]
    image_map = jnp.concatenate([
        image_map[:, :block] - through_own[:16],
        image_map[:, block:dofs - block],
        image_map[:, dofs - block:] + through_next[16:] - through_next[:16],
    ], axis=1)
    second_map = apply_rows(image_map, stiff_high[...], stiff_low[...])
    second_map = jnp.concatenate([
        second_map[:, :block] - own_rows(prev_image),
        second_map[:, block:dofs - block],
        second_map[:, dofs - block:] - next_rows(next_image),
    ], axis=1)
    basis = jnp.concatenate([maps, image_map, second_map, cubic], axis=0)
    gram_buf[part, 0:32] = dot_nt(
        basis[0:32], jnp.concatenate([basis[0:48], jnp.zeros((LANES - 48, dofs), F32)], axis=0),
        HIGHEST,
    )
    gram_buf[part, 32:48] = ends(second_map)
    gram_copies = share(gram_buf, gram_send, gram_recv)
    sends += gram_copies

    basis_cols = jnp.transpose(basis)
    arrive(point_copies)

    def compact(rows):
        rows = rows.reshape(places, LANES)
        if padded == capacity:
            return rows
        row, col = iota((columns, places), 0), iota((columns, places), 1)
        take = (col == (row // capacity) * padded + row % capacity).astype(F32)
        return jnp.dot(take, rows, precision=HIGHEST, preferred_element_type=F32)

    received = jnp.transpose(compact(in_points[...]))[:16]
    flag = received[comps:comps + 1]
    strain = jnp.where(iota((16, columns), 0) < comps, received, 0.0)
    hard = basis_cols[:, 48:49] * flag

    arrive(gram_copies)
    ghost_basis = jnp.concatenate([
        jnp.concatenate([prev_map, next_map], axis=1),
        jnp.concatenate([prev_image, next_image], axis=1),
        jnp.concatenate(
            [gram_buf[behind, 32:48][:, block:], gram_buf[after, 32:48][:, :block]], axis=1
        ),
        jnp.concatenate([prev_edge[32:48, block:], next_edge[32:48, :block]], axis=1),
    ], axis=0)
    ghost_cols = jnp.transpose(ghost_basis)
    ghost_hard = ghost_cols[:, 48:49] * flag
    gram = gathered(gram_buf)
    forms = jnp.concatenate(
        [gram[0:16, 0:16], gram[0:16, 16:32], gram[16:32, 16:32], gram[16:32, 32:48]], axis=0
    )
    forms = jnp.dot(forms, strain, precision=HIGHEST, preferred_element_type=F32)
    norm = col_sum(forms[0:16] * strain)
    curve = col_sum(forms[16:32] * strain)
    third = col_sum(forms[32:48] * strain)
    fourth = col_sum(forms[48:64] * strain)

    def second_step(norm, curve, left_norm, left_curve, cross):
        ratio = left_norm / (norm + EPSILON)
        next_curve = left_curve + ratio * (2.0 * cross + ratio * curve)
        next_curve = jnp.maximum(next_curve, 0.09 * left_norm)
        next_len = left_norm / (next_curve + EPSILON)
        return next_len, next_len * ratio

    step_len = norm / (curve + EPSILON)
    left_norm = jnp.maximum(norm - step_len * (2.0 * curve - step_len * third), 0.0)
    left_curve = curve - step_len * (2.0 * third - step_len * fourth)
    cross = curve - step_len * third
    next_len, carried = second_step(norm, curve, left_norm, left_curve, cross)
    along = step_len + carried + next_len
    across = next_len * step_len
    zero = jnp.zeros_like(strain)
    weights = jnp.concatenate([
        jnp.concatenate([along * strain, -across * strain, zero], axis=0),
        jnp.concatenate([strain, -along * strain, across * strain], axis=0),
    ], axis=1)
    both = jnp.dot(
        jnp.concatenate([basis_cols[:, :48], ghost_cols[:, :48]], axis=0), weights,
        precision=HIGHEST, preferred_element_type=F32,
    )
    solved = both[:dofs, :columns]
    hard_square = hard * solved * solved
    tangent = 3.0 * hard_square
    residue = both[:dofs, columns:] - hard_square * solved
    ghost_solved = both[dofs:, :columns]
    ghost = both[dofs:, columns:] - ghost_hard * ghost_solved * ghost_solved * ghost_solved

    def coupled(product, ghost):
        top = product[:block] - apply_split(own_high, own_low, ghost[:block])
        bottom = product[dofs - block:] - apply_split(next_high, next_low, ghost[block:])
        return jnp.concatenate([top, product[block:dofs - block], bottom], axis=0)

    def averaged(values):
        return apply_split(average_high, average_low, values)[:comps]

    image = coupled(apply_split(stiff_high[...], stiff_low[...], residue), ghost)
    image = image + tangent * residue
    halo_out[0] = image[:block]
    halo_out[1] = image[dofs - block:]
    halo_copies = to_neighbours(
        halo_out.at[0], halo_out.at[1], halo_in, halo_send, halo_recv
    )
    first_buf[part] = pad_rows(jnp.concatenate([
        averaged(solved), averaged(residue), averaged(image),
        col_sum(residue * residue), col_sum(residue * image),
    ], axis=0), first_buf.shape[1])
    first_copies = share(first_buf, first_send, first_recv)
    sends += halo_copies + first_copies
    second = apply_split(stiff_high[...], stiff_low[...], image)
    arrive(first_copies)
    sums = gathered(first_buf)
    norm, curve = sums[3 * comps:3 * comps + 1], sums[3 * comps + 1:3 * comps + 2]
    step_len = norm / (curve + EPSILON)
    left = residue - step_len * image
    arrive(halo_copies)
    second = coupled(second, halo_in[...].reshape(2 * block, columns)) + tangent * image
    left_image = image - step_len * second
    second_buf[part] = pad_rows(jnp.concatenate(
        [col_sum(left * left), col_sum(left * left_image), col_sum(left * image)], axis=0
    ), 8)
    second_copies = share(second_buf, second_send, second_recv)
    sends += second_copies
    arrive(second_copies)
    last = gathered(second_buf)
    next_len, carried = second_step(norm, curve, last[0:1], last[1:2], last[2:3])
    along = step_len + carried
    total = (
        sums[:comps] + along * sums[comps:2 * comps]
        + next_len * (sums[comps:2 * comps] - step_len * sums[2 * comps:3 * comps])
    )

    rows = jnp.transpose(pad_rows(total, LANES))
    if padded != capacity:
        row, col = iota((places, columns), 0), iota((places, columns), 1)
        spread = jnp.logical_and(
            col == (row // padded) * capacity + row % padded, row % padded < capacity
        ).astype(F32)
        rows = jnp.dot(spread, rows, precision=HIGHEST, preferred_element_type=F32)
    out_rows[...] = rows.reshape(groups, padded, LANES)
    row_copies = exchange(out_rows, in_rows, row_send, row_recv)
    sends += row_copies
    in_rows[group] = out_rows[group]
    field_ref[0] = solved + along * residue + next_len * left
    arrive(row_copies)
    back = jnp.transpose(in_rows[...].reshape(places, LANES))[:16]
    picked = jnp.dot(back, select, precision=HIGHEST, preferred_element_type=F32)
    stress_ref[...] = picked[:comps]
    for copy in sends:
        copy.wait_send()


def solution(mesh):
    groups, parts = mesh.shape["macro"], mesh.shape["rve"]

    def shards(deform, plastic, route, stiff, cubic, coupling, conn, iface, load_map, average_map):
        comps, points = deform.shape
        blocks, block = coupling.shape[1], coupling.shape[3]
        dofs = blocks * block
        capacity = 2 * points // groups
        columns = groups * capacity
        padded = -(-capacity // 8) * 8
        vmem = pl.BlockSpec(memory_space=pltpu.VMEM)
        hbm = pl.BlockSpec(memory_space=pltpu.HBM)
        dma = pltpu.SemaphoreType.DMA
        return pl.pallas_call(
            functools.partial(kernel, groups, parts, capacity),
            out_shape=(
                jax.ShapeDtypeStruct((comps, points), F32),
                jax.ShapeDtypeStruct((1, dofs, columns), F32),
            ),
            in_specs=[hbm] * 6 + [pl.BlockSpec(memory_space=pltpu.SMEM)] + [hbm] * 3,
            out_specs=(vmem, vmem),
            scratch_shapes=[
                pltpu.VMEM(deform.shape, F32),
                pltpu.VMEM((1, points), jnp.int32),
                pltpu.VMEM((1, points), jnp.int32),
                pltpu.VMEM((1, dofs), F32),
                pltpu.VMEM((1, dofs), F32),
                pltpu.VMEM(coupling.shape, F32),
                pltpu.VMEM(iface.shape, F32),
                pltpu.VMEM((comps, 1, dofs), F32),
                pltpu.VMEM((comps, 1, dofs), F32),
                pltpu.VMEM((dofs, dofs), F32),
                pltpu.VMEM((dofs, dofs), BF16),
                pltpu.VMEM((dofs, dofs), BF16),
                pltpu.VMEM((groups, padded, LANES), F32),
                pltpu.VMEM((groups, padded, LANES), F32),
                pltpu.VMEM((48 + block // 2, LANES), F32),
                pltpu.VMEM((2, 48 + block // 2, LANES), F32),
                pltpu.VMEM((2, block, columns), F32),
                pltpu.VMEM((2, block, columns), F32),
                pltpu.VMEM((parts, 48, LANES), F32),
                pltpu.VMEM((parts, 32, columns), F32),
                pltpu.VMEM((parts, 8, columns), F32),
                pltpu.VMEM((groups, padded, LANES), F32),
                pltpu.VMEM((groups, padded, LANES), F32),
                dma((9,)),
                dma((groups - 1,)), dma((groups - 1,)),
                dma((2,)), dma((2,)),
                dma((2,)), dma((2,)),
                dma((parts - 1,)), dma((parts - 1,)),
                dma((parts - 1,)), dma((parts - 1,)),
                dma((parts - 1,)), dma((parts - 1,)),
                dma((groups - 1,)), dma((groups - 1,)),
            ],
            compiler_params=pltpu.CompilerParams(
                collective_id=0, has_side_effects=True, vmem_limit_bytes=60 * 1024 * 1024
            ),
        )(
            deform, plastic[None], route[None], stiff, cubic, coupling,
            jnp.transpose(conn, (0, 2, 1)), iface,
            jnp.transpose(load_map, (1, 0, 2)), jnp.transpose(average_map, (1, 0, 2)),
        )

    return jax.shard_map(
        shards,
        mesh=mesh,
        in_specs=(
            P(None, "macro"),
            P("macro"),
            P("macro"),
            P("macro", "rve"),
            P("macro", "rve"),
            P("macro", "rve", None, None, None),
            P("macro", "rve", None),
            P("macro", "rve", None),
            P("macro", None, "rve"),
            P("macro", None, "rve"),
        ),
        out_specs=(P(None, "macro"), P("macro", "rve", None)),
        check_vma=False,
    )
```

```python
import functools

import jax
import jax.numpy as jnp
from jax import lax
from jax.experimental import pallas as pl
from jax.experimental.pallas import tpu as pltpu
from jax.sharding import PartitionSpec as P

EPSILON = 1e-06
MESH = pl.DeviceIdType.MESH
HIGHEST = lax.Precision.HIGHEST
F32 = jnp.float32
BF16 = jnp.bfloat16
LANES = 128
NT = (((1,), (1,)), ((), ()))


def split(values):
    high = values.astype(BF16)
    return high, (values - high.astype(F32)).astype(BF16)


def dot(left, right):
    return jnp.dot(left, right, preferred_element_type=F32)


def dot_nt(left, right, precision=None):
    return lax.dot_general(left, right, NT, precision=precision, preferred_element_type=F32)


def apply_split(high, low, values):
    value_high, value_low = split(values)
    width = values.shape[1]
    wide = dot(high, jnp.concatenate([value_high, value_low], axis=1))
    return wide[:, :width] + wide[:, width:] + dot(low, value_high)


def apply_rows(values, high, low):
    value_high, value_low = split(values)
    rows = values.shape[0]
    tall = dot(jnp.concatenate([value_high, value_low], axis=0), high)
    return tall[:rows] + tall[rows:] + dot(value_high, low)


def square_nt(values):
    high, low = split(values)
    return dot_nt(high, high) + (dot_nt(high, low) + dot_nt(low, high))


def iota(shape, dim):
    return lax.broadcasted_iota(jnp.int32, shape, dim)


def pad_rows(values, rows):
    missing = rows - values.shape[0]
    if missing == 0:
        return values
    return jnp.concatenate([values, jnp.zeros((missing, values.shape[1]), values.dtype)], axis=0)


def col_sum(values):
    return jnp.sum(values, axis=0, keepdims=True)


def kernel(
    groups, parts, capacity,
    deform_hbm, plastic_hbm, route_hbm, stiff_hbm, cubic_hbm, coupling_hbm, conn_ref,
    iface_hbm, load_hbm, average_hbm,
    stress_ref, field_ref,
    deform_ref, plastic_ref, route_ref, stiff_ref, cubic_ref, coupling_ref,
    iface_ref, load_ref, average_ref,
    whole, stiff_high, stiff_low,
    out_points, in_points, edge_out, edge_in,
    halo_out, halo_in, gram_buf, first_buf, mean_buf, second_buf, out_rows, in_rows, field_buf,
    input_sem, output_sem,
    point_send, point_recv, edge_send, edge_recv, halo_send, halo_recv,
    gram_send, gram_recv, first_send, first_recv, mean_send, mean_recv, second_send, second_recv, row_send, row_recv,
):
    group = lax.axis_index("macro")
    part = lax.axis_index("rve")
    blocks, slots, block = coupling_ref.shape[1], coupling_ref.shape[2], coupling_ref.shape[3]
    dofs = blocks * block
    comps, points = deform_ref.shape
    padded = out_points.shape[1]
    columns = groups * capacity
    places = groups * padded

    barrier = pltpu.get_barrier_semaphore()
    for step in range(1, parts):
        pl.semaphore_signal(
            barrier, inc=1, device_id={"rve": lax.rem(part + step, parts)}, device_id_type=MESH
        )
    for step in range(1, groups):
        pl.semaphore_signal(
            barrier, inc=1, device_id={"macro": lax.rem(group + step, groups)}, device_id_type=MESH
        )

    loads = []
    for source, target in (
        (coupling_hbm, coupling_ref), (iface_hbm, iface_ref), (load_hbm, load_ref),
        (cubic_hbm, cubic_ref), (stiff_hbm, stiff_ref), (deform_hbm, deform_ref),
        (plastic_hbm, plastic_ref), (route_hbm, route_ref), (average_hbm, average_ref),
    ):
        loads.append(pltpu.make_async_copy(source, target, input_sem.at[len(loads)]))
        loads[-1].start()
    coupling_load, iface_load = loads[:2]
    early_loads, late_loads = loads[2:5], loads[5:]

    def exchange(source, target, send, recv):
        copies = []
        for step in range(1, groups):
            peer = lax.rem(group + step, groups)
            copies.append(pltpu.make_async_remote_copy(
                src_ref=source.at[peer], dst_ref=target.at[group],
                send_sem=send.at[step - 1], recv_sem=recv.at[step - 1],
                device_id={"macro": peer}, device_id_type=MESH,
            ))
            copies[-1].start()
        return copies

    def share(buffer, send, recv):
        copies = []
        for step in range(1, parts):
            copies.append(pltpu.make_async_remote_copy(
                src_ref=buffer.at[part], dst_ref=buffer.at[part],
                send_sem=send.at[step - 1], recv_sem=recv.at[step - 1],
                device_id={"rve": lax.rem(part + step, parts)}, device_id_type=MESH,
            ))
            copies[-1].start()
        return copies

    after, behind = lax.rem(part + 1, parts), lax.rem(part + parts - 1, parts)

    def to_neighbours(first, last, target, send, recv):
        copies = []
        for place, (source, peer) in enumerate(((last, after), (first, behind))):
            copies.append(pltpu.make_async_remote_copy(
                src_ref=source, dst_ref=target.at[place],
                send_sem=send.at[place], recv_sem=recv.at[place],
                device_id={"rve": peer}, device_id_type=MESH,
            ))
            copies[-1].start()
        return copies

    def arrive(copies):
        for copy in copies:
            copy.wait_recv()

    def gathered(buffer):
        total = buffer[0]
        for other in range(1, parts):
            total = total + buffer[other]
        return total

    coupling_load.wait()
    lane = iota((block, LANES), 1) < block
    doubled = []
    for row in range(blocks):
        square = square_nt(coupling_ref[0, row].reshape(slots * block, block))
        doubled.append([])
        for slot in range(slots):
            spring = square[slot * block:(slot + 1) * block, slot * block:(slot + 1) * block]
            doubled[row].append(jnp.concatenate([spring, spring], axis=1))

    def mark(row, slot, far):
        if row == far:
            return jnp.float32(0.0)
        return jnp.where(conn_ref[0, slot, row] == far, 1.0, 0.0).astype(F32)

    for row in range(blocks):
        own = doubled[row][0]
        for slot in range(1, slots):
            own = own + doubled[row][slot]
        for other in range(blocks):
            if other != row:
                for slot in range(slots):
                    own = own + doubled[other][slot] * mark(other, slot, row)
        for pair in range(blocks // 2):
            left, right = 2 * pair, 2 * pair + 1
            value = jnp.zeros((block, LANES), F32)
            for slot in range(slots):
                value = value - doubled[row][slot] * jnp.where(
                    lane, mark(row, slot, left), mark(row, slot, right)
                )
                value = value - jnp.where(
                    lane, doubled[left][slot] * mark(left, slot, row),
                    doubled[right][slot] * mark(right, slot, row),
                )
            if row == left:
                value = value + jnp.where(lane, own, 0.0)
            if row == right:
                value = value + jnp.where(lane, 0.0, own)
            whole[row * block:(row + 1) * block, pair * LANES:(pair + 1) * LANES] = value

    iface_load.wait()
    for copy in early_loads:
        copy.wait()
    own_edge = iface_ref[0]
    own_spring = square_nt(own_edge)
    own_high, own_low = split(own_spring)
    diagonal = iota((dofs, dofs), 0) == iota((dofs, dofs), 1)
    stiffness = whole[...] + jnp.where(diagonal, stiff_ref[...], 0.0)
    high, low = split(stiffness)
    stiff_high[...] = high
    stiff_low[...] = low
    high, low = split(stiffness[:block, :block] + own_spring)
    stiff_high[:block, :block] = high
    stiff_low[:block, :block] = low

    maps = pad_rows(load_ref[:, 0, :], 16)
    cubic = pad_rows(cubic_ref[...], 16)

    def ends(values):
        return jnp.concatenate([values[:, :block], values[:, dofs - block:]], axis=1)

    image_map = apply_rows(maps, stiff_high[...], stiff_low[...])
    edge_out[0:16, :] = ends(maps)
    edge_out[16:32, :] = ends(image_map)
    edge_out[32:48, :] = ends(cubic)
    edge_out[48:, :] = jnp.concatenate([own_edge[:block // 2], own_edge[block // 2:]], axis=1)

    pl.semaphore_wait(barrier, groups + parts - 2)

    sends = []
    edge_copies = to_neighbours(edge_out, edge_out, edge_in, edge_send, edge_recv)

    for copy in late_loads:
        copy.wait()
    route = route_ref[...]
    hot = (iota((groups, points), 0) == route).astype(F32)
    before = (iota((points, points), 0) < iota((points, points), 1)).astype(BF16)
    rank = col_sum(hot * dot(hot.astype(BF16), before))
    slot_of = (route * padded).astype(F32) + rank
    select = (iota((places, points), 0).astype(F32) == slot_of).astype(F32)
    sent = pad_rows(
        jnp.concatenate([deform_ref[...], plastic_ref[...].astype(F32)], axis=0), LANES
    )
    outgoing = dot_nt(select, sent, HIGHEST)
    out_points[...] = outgoing.reshape(groups, padded, LANES)
    point_copies = exchange(out_points, in_points, point_send, point_recv)
    sends += point_copies + edge_copies
    in_points[group] = out_points[group]
    average_high, average_low = split(pad_rows(average_ref[:, 0, :], 16))

    arrive(edge_copies)
    packed = edge_in[1, 48:, :]
    next_spring = square_nt(jnp.concatenate([packed[:, :block], packed[:, block:]], axis=0))
    next_high, next_low = split(next_spring)
    high, low = split(stiffness[dofs - block:, dofs - block:] + next_spring)
    stiff_high[dofs - block:, dofs - block:] = high
    stiff_low[dofs - block:, dofs - block:] = low

    def own_rows(values):
        return apply_rows(values, own_high, own_low)

    def next_rows(values):
        return apply_rows(values, next_high, next_low)

    prev_edge, next_edge = edge_in[0], edge_in[1]
    prev_map, next_map = prev_edge[0:16, block:], next_edge[0:16, :block]
    first_map, last_map = maps[:, :block], maps[:, dofs - block:]
    through_own = own_rows(jnp.concatenate([prev_map, first_map], axis=0))
    through_next = next_rows(jnp.concatenate([next_map, last_map], axis=0))
    prev_image = prev_edge[16:32, block:] + through_own[:16] - through_own[16:]
    next_image = next_edge[16:32, :block] - through_next[16:]
    image_map = jnp.concatenate([
        image_map[:, :block] - through_own[:16],
        image_map[:, block:dofs - block],
        image_map[:, dofs - block:] + through_next[16:] - through_next[:16],
    ], axis=1)
    second_map = apply_rows(image_map, stiff_high[...], stiff_low[...])
    second_map = jnp.concatenate([
        second_map[:, :block] - own_rows(prev_image),
        second_map[:, block:dofs - block],
        second_map[:, dofs - block:] - next_rows(next_image),
    ], axis=1)
    basis = jnp.concatenate([maps, image_map, second_map, cubic], axis=0)
    gram_buf[part, 0:32] = dot_nt(
        basis[0:32], jnp.concatenate([basis[0:48], jnp.zeros((LANES - 48, dofs), F32)], axis=0),
        HIGHEST,
    )
    gram_buf[part, 32:48] = ends(second_map)
    gram_copies = share(gram_buf, gram_send, gram_recv)
    sends += gram_copies

    basis_cols = jnp.transpose(basis)
    arrive(point_copies)

    def compact(rows):
        rows = rows.reshape(places, LANES)
        if padded == capacity:
            return rows
        row, col = iota((columns, places), 0), iota((columns, places), 1)
        take = (col == (row // capacity) * padded + row % capacity).astype(F32)
        return jnp.dot(take, rows, precision=HIGHEST, preferred_element_type=F32)

    received = jnp.transpose(compact(in_points[...]))[:16]
    flag = received[comps:comps + 1]
    strain = jnp.where(iota((16, columns), 0) < comps, received, 0.0)
    hard = basis_cols[:, 48:49] * flag

    arrive(gram_copies)
    ghost_basis = jnp.concatenate([
        jnp.concatenate([prev_map, next_map], axis=1),
        jnp.concatenate([prev_image, next_image], axis=1),
        jnp.concatenate(
            [gram_buf[behind, 32:48][:, block:], gram_buf[after, 32:48][:, :block]], axis=1
        ),
        jnp.concatenate([prev_edge[32:48, block:], next_edge[32:48, :block]], axis=1),
    ], axis=0)
    ghost_cols = jnp.transpose(ghost_basis)
    ghost_hard = ghost_cols[:, 48:49] * flag
    gram = gathered(gram_buf)
    forms = jnp.concatenate(
        [gram[0:16, 0:16], gram[0:16, 16:32], gram[16:32, 16:32], gram[16:32, 32:48]], axis=0
    )
    forms = jnp.dot(forms, strain, precision=HIGHEST, preferred_element_type=F32)
    norm = col_sum(forms[0:16] * strain)
    curve = col_sum(forms[16:32] * strain)
    third = col_sum(forms[32:48] * strain)
    fourth = col_sum(forms[48:64] * strain)

    def second_step(norm, curve, left_norm, left_curve, cross):
        ratio = left_norm / (norm + EPSILON)
        next_curve = left_curve + ratio * (2.0 * cross + ratio * curve)
        next_curve = jnp.maximum(next_curve, 0.09 * left_norm)
        next_len = left_norm / (next_curve + EPSILON)
        return next_len, next_len * ratio

    step_len = norm / (curve + EPSILON)
    left_norm = jnp.maximum(norm - step_len * (2.0 * curve - step_len * third), 0.0)
    left_curve = curve - step_len * (2.0 * third - step_len * fourth)
    cross = curve - step_len * third
    next_len, carried = second_step(norm, curve, left_norm, left_curve, cross)
    along = step_len + carried + next_len
    across = next_len * step_len
    zero = jnp.zeros_like(strain)
    weights = jnp.concatenate([
        jnp.concatenate([along * strain, -across * strain, zero], axis=0),
        jnp.concatenate([strain, -along * strain, across * strain], axis=0),
    ], axis=1)
    both = jnp.dot(
        jnp.concatenate([basis_cols[:, :48], ghost_cols[:, :48]], axis=0), weights,
        precision=HIGHEST, preferred_element_type=F32,
    )
    solved = both[:dofs, :columns]
    hard_square = hard * solved * solved
    tangent = 3.0 * hard_square
    residue = both[:dofs, columns:] - hard_square * solved
    ghost_solved = both[dofs:, :columns]
    ghost = both[dofs:, columns:] - ghost_hard * ghost_solved * ghost_solved * ghost_solved

    def coupled(product, ghost):
        top = product[:block] - apply_split(own_high, own_low, ghost[:block])
        bottom = product[dofs - block:] - apply_split(next_high, next_low, ghost[block:])
        return jnp.concatenate([top, product[block:dofs - block], bottom], axis=0)

    def averaged(values):
        return apply_split(average_high, average_low, values)[:comps]

    image = coupled(apply_split(stiff_high[...], stiff_low[...], residue), ghost)
    image = image + tangent * residue
    halo_out[0] = image[:block]
    halo_out[1] = image[dofs - block:]
    halo_copies = to_neighbours(
        halo_out.at[0], halo_out.at[1], halo_in, halo_send, halo_recv
    )
    first_buf[part] = pad_rows(jnp.concatenate([
        col_sum(residue * residue), col_sum(residue * image),
    ], axis=0), first_buf.shape[1])
    first_copies = share(first_buf, first_send, first_recv)
    second = apply_split(stiff_high[...], stiff_low[...], image)
    mean_buf[part] = pad_rows(jnp.concatenate(
        [averaged(solved), averaged(residue), averaged(image)], axis=0
    ), mean_buf.shape[1])
    mean_copies = share(mean_buf, mean_send, mean_recv)
    sends += halo_copies + first_copies + mean_copies
    arrive(first_copies)
    sums = gathered(first_buf)
    norm, curve = sums[0:1], sums[1:2]
    step_len = norm / (curve + EPSILON)
    left = residue - step_len * image
    arrive(halo_copies)
    second = coupled(second, halo_in[...].reshape(2 * block, columns)) + tangent * image
    left_image = image - step_len * second
    second_buf[part] = pad_rows(jnp.concatenate(
        [col_sum(left * left), col_sum(left * left_image), col_sum(left * image)], axis=0
    ), 8)
    second_copies = share(second_buf, second_send, second_recv)
    sends += second_copies
    arrive(mean_copies)
    means = gathered(mean_buf)
    arrive(second_copies)
    last = gathered(second_buf)
    next_len, carried = second_step(norm, curve, last[0:1], last[1:2], last[2:3])
    along = step_len + carried
    total = (
        means[:comps] + along * means[comps:2 * comps]
        + next_len * (means[comps:2 * comps] - step_len * means[2 * comps:3 * comps])
    )

    rows = jnp.transpose(pad_rows(total, LANES))
    if padded != capacity:
        row, col = iota((places, columns), 0), iota((places, columns), 1)
        spread = jnp.logical_and(
            col == (row // padded) * capacity + row % padded, row % padded < capacity
        ).astype(F32)
        rows = jnp.dot(spread, rows, precision=HIGHEST, preferred_element_type=F32)
    out_rows[...] = rows.reshape(groups, padded, LANES)
    row_copies = exchange(out_rows, in_rows, row_send, row_recv)
    sends += row_copies
    in_rows[group] = out_rows[group]
    field_buf[0] = solved + along * residue + next_len * left
    field_copy = pltpu.make_async_copy(field_buf, field_ref, output_sem)
    field_copy.start()
    arrive(row_copies)
    back = jnp.transpose(in_rows[...].reshape(places, LANES))[:16]
    picked = jnp.dot(back, select, precision=HIGHEST, preferred_element_type=F32)
    stress_ref[...] = picked[:comps]
    for copy in sends:
        copy.wait_send()
    field_copy.wait()


def solution(mesh):
    groups, parts = mesh.shape["macro"], mesh.shape["rve"]

    def shards(deform, plastic, route, stiff, cubic, coupling, conn, iface, load_map, average_map):
        comps, points = deform.shape
        blocks, block = coupling.shape[1], coupling.shape[3]
        dofs = blocks * block
        capacity = 2 * points // groups
        columns = groups * capacity
        padded = -(-capacity // 8) * 8
        vmem = pl.BlockSpec(memory_space=pltpu.VMEM)
        hbm = pl.BlockSpec(memory_space=pltpu.HBM)
        dma = pltpu.SemaphoreType.DMA
        return pl.pallas_call(
            functools.partial(kernel, groups, parts, capacity),
            out_shape=(
                jax.ShapeDtypeStruct((comps, points), F32),
                jax.ShapeDtypeStruct((1, dofs, columns), F32),
            ),
            in_specs=[hbm] * 6 + [pl.BlockSpec(memory_space=pltpu.SMEM)] + [hbm] * 3,
            out_specs=(vmem, hbm),
            scratch_shapes=[
                pltpu.VMEM(deform.shape, F32),
                pltpu.VMEM((1, points), jnp.int32),
                pltpu.VMEM((1, points), jnp.int32),
                pltpu.VMEM((1, dofs), F32),
                pltpu.VMEM((1, dofs), F32),
                pltpu.VMEM(coupling.shape, F32),
                pltpu.VMEM(iface.shape, F32),
                pltpu.VMEM((comps, 1, dofs), F32),
                pltpu.VMEM((comps, 1, dofs), F32),
                pltpu.VMEM((dofs, dofs), F32),
                pltpu.VMEM((dofs, dofs), BF16),
                pltpu.VMEM((dofs, dofs), BF16),
                pltpu.VMEM((groups, padded, LANES), F32),
                pltpu.VMEM((groups, padded, LANES), F32),
                pltpu.VMEM((48 + block // 2, LANES), F32),
                pltpu.VMEM((2, 48 + block // 2, LANES), F32),
                pltpu.VMEM((2, block, columns), F32),
                pltpu.VMEM((2, block, columns), F32),
                pltpu.VMEM((parts, 48, LANES), F32),
                pltpu.VMEM((parts, 8, columns), F32),
                pltpu.VMEM((parts, 32, columns), F32),
                pltpu.VMEM((parts, 8, columns), F32),
                pltpu.VMEM((groups, padded, LANES), F32),
                pltpu.VMEM((groups, padded, LANES), F32),
                pltpu.VMEM((1, dofs, columns), F32),
                dma((9,)), dma,
                dma((groups - 1,)), dma((groups - 1,)),
                dma((2,)), dma((2,)),
                dma((2,)), dma((2,)),
                dma((parts - 1,)), dma((parts - 1,)),
                dma((parts - 1,)), dma((parts - 1,)),
                dma((parts - 1,)), dma((parts - 1,)),
                dma((parts - 1,)), dma((parts - 1,)),
                dma((groups - 1,)), dma((groups - 1,)),
            ],
            compiler_params=pltpu.CompilerParams(
                collective_id=0, has_side_effects=True, vmem_limit_bytes=60 * 1024 * 1024
            ),
        )(
            deform, plastic[None], route[None], stiff, cubic, coupling,
            jnp.transpose(conn, (0, 2, 1)), iface,
            jnp.transpose(load_map, (1, 0, 2)), jnp.transpose(average_map, (1, 0, 2)),
        )

    return jax.shard_map(
        shards,
        mesh=mesh,
        in_specs=(
            P(None, "macro"),
            P("macro"),
            P("macro"),
            P("macro", "rve"),
            P("macro", "rve"),
            P("macro", "rve", None, None, None),
            P("macro", "rve", None),
            P("macro", "rve", None),
            P("macro", None, "rve"),
            P("macro", None, "rve"),
        ),
        out_specs=(P(None, "macro"), P("macro", "rve", None)),
        check_vma=False,
    )
```

```python
import functools

import jax
import jax.numpy as jnp
from jax import lax
from jax.experimental import pallas as pl
from jax.experimental.pallas import tpu as pltpu
from jax.sharding import PartitionSpec as P

EPSILON = 1e-06
MESH = pl.DeviceIdType.MESH
HIGHEST = lax.Precision.HIGHEST
F32 = jnp.float32
BF16 = jnp.bfloat16
LANES = 128
NT = (((1,), (1,)), ((), ()))


def split(values):
    high = values.astype(BF16)
    return high, (values - high.astype(F32)).astype(BF16)


def dot(left, right):
    return jnp.dot(left, right, preferred_element_type=F32)


def dot_nt(left, right, precision=None):
    return lax.dot_general(left, right, NT, precision=precision, preferred_element_type=F32)


def apply_split(high, low, values):
    value_high, value_low = split(values)
    width = values.shape[1]
    wide = dot(high, jnp.concatenate([value_high, value_low], axis=1))
    return wide[:, :width] + wide[:, width:] + dot(low, value_high)


def apply_rows(values, high, low):
    value_high, value_low = split(values)
    rows = values.shape[0]
    tall = dot(jnp.concatenate([value_high, value_low], axis=0), high)
    return tall[:rows] + tall[rows:] + dot(value_high, low)


def square_nt(values):
    high, low = split(values)
    return dot_nt(high, high) + (dot_nt(high, low) + dot_nt(low, high))


def iota(shape, dim):
    return lax.broadcasted_iota(jnp.int32, shape, dim)


def pad_rows(values, rows):
    missing = rows - values.shape[0]
    if missing == 0:
        return values
    return jnp.concatenate([values, jnp.zeros((missing, values.shape[1]), values.dtype)], axis=0)


def col_sum(values):
    return jnp.sum(values, axis=0, keepdims=True)


def kernel(
    groups, parts, capacity,
    deform_hbm, plastic_hbm, route_hbm, stiff_hbm, cubic_hbm, coupling_hbm, conn_ref,
    iface_hbm, load_hbm, average_hbm,
    stress_ref, field_ref,
    deform_ref, plastic_ref, route_ref, stiff_ref, cubic_ref, coupling_ref,
    iface_ref, load_ref, average_ref,
    whole, stiff_high, stiff_low,
    out_points, in_points, edge_out, edge_in,
    halo_out, halo_in, gram_buf, first_buf, mean_buf, second_buf, out_rows, in_rows, field_buf,
    input_sem, output_sem,
    point_send, point_recv, edge_send, edge_recv, halo_send, halo_recv,
    gram_send, gram_recv, first_send, first_recv, mean_send, mean_recv, second_send, second_recv, row_send, row_recv,
):
    group = lax.axis_index("macro")
    part = lax.axis_index("rve")
    blocks, slots, block = coupling_ref.shape[1], coupling_ref.shape[2], coupling_ref.shape[3]
    dofs = blocks * block
    comps, points = deform_ref.shape
    padded = out_points.shape[1]
    columns = groups * capacity
    places = groups * padded

    barrier = pltpu.get_barrier_semaphore()
    for step in range(1, parts):
        pl.semaphore_signal(
            barrier, inc=1, device_id={"rve": lax.rem(part + step, parts)}, device_id_type=MESH
        )
    for step in range(1, groups):
        pl.semaphore_signal(
            barrier, inc=1, device_id={"macro": lax.rem(group + step, groups)}, device_id_type=MESH
        )

    loads = []
    for source, target in (
        (coupling_hbm, coupling_ref), (iface_hbm, iface_ref), (load_hbm, load_ref),
        (cubic_hbm, cubic_ref), (stiff_hbm, stiff_ref), (deform_hbm, deform_ref),
        (plastic_hbm, plastic_ref), (route_hbm, route_ref), (average_hbm, average_ref),
    ):
        loads.append(pltpu.make_async_copy(source, target, input_sem.at[len(loads)]))
        loads[-1].start()
    coupling_load, iface_load = loads[:2]
    early_loads, late_loads = loads[2:5], loads[5:]

    def exchange(source, target, send, recv):
        copies = []
        for step in range(1, groups):
            peer = lax.rem(group + step, groups)
            copies.append(pltpu.make_async_remote_copy(
                src_ref=source.at[peer], dst_ref=target.at[group],
                send_sem=send.at[step - 1], recv_sem=recv.at[step - 1],
                device_id={"macro": peer}, device_id_type=MESH,
            ))
            copies[-1].start()
        return copies

    def share(buffer, send, recv):
        copies = []
        for step in range(1, parts):
            copies.append(pltpu.make_async_remote_copy(
                src_ref=buffer.at[part], dst_ref=buffer.at[part],
                send_sem=send.at[step - 1], recv_sem=recv.at[step - 1],
                device_id={"rve": lax.rem(part + step, parts)}, device_id_type=MESH,
            ))
            copies[-1].start()
        return copies

    after, behind = lax.rem(part + 1, parts), lax.rem(part + parts - 1, parts)

    def to_neighbours(first, last, target, send, recv):
        copies = []
        for place, (source, peer) in enumerate(((last, after), (first, behind))):
            copies.append(pltpu.make_async_remote_copy(
                src_ref=source, dst_ref=target.at[place],
                send_sem=send.at[place], recv_sem=recv.at[place],
                device_id={"rve": peer}, device_id_type=MESH,
            ))
            copies[-1].start()
        return copies

    def arrive(copies):
        for copy in copies:
            copy.wait_recv()

    def gathered(buffer):
        total = buffer[0]
        for other in range(1, parts):
            total = total + buffer[other]
        return total

    coupling_load.wait()
    lane = iota((block, LANES), 1) < block
    doubled = []
    for row in range(blocks):
        square = square_nt(coupling_ref[0, row].reshape(slots * block, block))
        doubled.append([])
        for slot in range(slots):
            spring = square[slot * block:(slot + 1) * block, slot * block:(slot + 1) * block]
            doubled[row].append(jnp.concatenate([spring, spring], axis=1))

    def mark(row, slot, far):
        if row == far:
            return jnp.float32(0.0)
        return jnp.where(conn_ref[0, slot, row] == far, 1.0, 0.0).astype(F32)

    for row in range(blocks):
        own = doubled[row][0]
        for slot in range(1, slots):
            own = own + doubled[row][slot]
        for other in range(blocks):
            if other != row:
                for slot in range(slots):
                    own = own + doubled[other][slot] * mark(other, slot, row)
        for pair in range(blocks // 2):
            left, right = 2 * pair, 2 * pair + 1
            value = jnp.zeros((block, LANES), F32)
            for slot in range(slots):
                value = value - doubled[row][slot] * jnp.where(
                    lane, mark(row, slot, left), mark(row, slot, right)
                )
                value = value - jnp.where(
                    lane, doubled[left][slot] * mark(left, slot, row),
                    doubled[right][slot] * mark(right, slot, row),
                )
            if row == left:
                value = value + jnp.where(lane, own, 0.0)
            if row == right:
                value = value + jnp.where(lane, 0.0, own)
            whole[row * block:(row + 1) * block, pair * LANES:(pair + 1) * LANES] = value

    iface_load.wait()
    for copy in early_loads:
        copy.wait()
    own_edge = iface_ref[0]
    own_spring = square_nt(own_edge)
    own_high, own_low = split(own_spring)
    diagonal = iota((dofs, dofs), 0) == iota((dofs, dofs), 1)
    stiffness = whole[...] + jnp.where(diagonal, stiff_ref[...], 0.0)
    high, low = split(stiffness)
    stiff_high[...] = high
    stiff_low[...] = low
    high, low = split(stiffness[:block, :block] + own_spring)
    stiff_high[:block, :block] = high
    stiff_low[:block, :block] = low

    maps = pad_rows(load_ref[:, 0, :], 16)
    cubic = pad_rows(cubic_ref[...], 16)

    def ends(values):
        return jnp.concatenate([values[:, :block], values[:, dofs - block:]], axis=1)

    image_map = apply_rows(maps, stiff_high[...], stiff_low[...])
    packed_rows = edge_out.shape[0] - block // 2
    edge_out[:packed_rows, :] = pad_rows(
        ends(jnp.concatenate([maps[:comps], image_map[:comps], cubic[:1]], axis=0)), packed_rows
    )
    edge_out[packed_rows:, :] = jnp.concatenate([own_edge[:block // 2], own_edge[block // 2:]], axis=1)

    pl.semaphore_wait(barrier, groups + parts - 2)

    sends = []
    edge_copies = to_neighbours(edge_out, edge_out, edge_in, edge_send, edge_recv)

    for copy in late_loads:
        copy.wait()
    route = route_ref[...]
    hot = (iota((groups, points), 0) == route).astype(F32)
    before = (iota((points, points), 0) < iota((points, points), 1)).astype(BF16)
    rank = col_sum(hot * dot(hot.astype(BF16), before))
    slot_of = (route * padded).astype(F32) + rank
    select = (iota((places, points), 0).astype(F32) == slot_of).astype(F32)
    sent = pad_rows(
        jnp.concatenate([deform_ref[...], plastic_ref[...].astype(F32)], axis=0), LANES
    )
    outgoing = dot_nt(select, sent, HIGHEST)
    out_points[...] = outgoing.reshape(groups, padded, LANES)
    point_copies = exchange(out_points, in_points, point_send, point_recv)
    sends += point_copies + edge_copies
    in_points[group] = out_points[group]
    average_high, average_low = split(pad_rows(average_ref[:, 0, :], 16))

    arrive(edge_copies)
    packed = edge_in[1, packed_rows:, :]
    next_spring = square_nt(jnp.concatenate([packed[:, :block], packed[:, block:]], axis=0))
    next_high, next_low = split(next_spring)
    high, low = split(stiffness[dofs - block:, dofs - block:] + next_spring)
    stiff_high[dofs - block:, dofs - block:] = high
    stiff_low[dofs - block:, dofs - block:] = low

    def own_rows(values):
        return apply_rows(values, own_high, own_low)

    def next_rows(values):
        return apply_rows(values, next_high, next_low)

    def unpack(values):
        return jnp.concatenate([
            pad_rows(values[:comps], 16), pad_rows(values[comps:2 * comps], 16),
            pad_rows(values[2 * comps:2 * comps + 1], 16),
        ], axis=0)

    prev_edge, next_edge = unpack(edge_in[0, :packed_rows]), unpack(edge_in[1, :packed_rows])
    prev_map, next_map = prev_edge[0:16, block:], next_edge[0:16, :block]
    first_map, last_map = maps[:, :block], maps[:, dofs - block:]
    through_own = own_rows(jnp.concatenate([prev_map, first_map], axis=0))
    through_next = next_rows(jnp.concatenate([next_map, last_map], axis=0))
    prev_image = prev_edge[16:32, block:] + through_own[:16] - through_own[16:]
    next_image = next_edge[16:32, :block] - through_next[16:]
    image_map = jnp.concatenate([
        image_map[:, :block] - through_own[:16],
        image_map[:, block:dofs - block],
        image_map[:, dofs - block:] + through_next[16:] - through_next[:16],
    ], axis=1)
    second_map = apply_rows(image_map, stiff_high[...], stiff_low[...])
    second_map = jnp.concatenate([
        second_map[:, :block] - own_rows(prev_image),
        second_map[:, block:dofs - block],
        second_map[:, dofs - block:] - next_rows(next_image),
    ], axis=1)
    basis = jnp.concatenate([maps, image_map, second_map, cubic], axis=0)
    products = dot_nt(basis[0:32], basis[0:48], HIGHEST)
    gram_buf[part, 0:16] = jnp.concatenate(
        [products[0:16, 0:32], products[16:32, 16:48], jnp.zeros((16, LANES - 64), F32)], axis=1
    )
    gram_buf[part, 16:32] = ends(second_map)
    gram_copies = share(gram_buf, gram_send, gram_recv)
    sends += gram_copies

    basis_cols = jnp.transpose(basis)
    arrive(point_copies)

    def compact(rows):
        rows = rows.reshape(places, LANES)
        if padded == capacity:
            return rows
        row, col = iota((columns, places), 0), iota((columns, places), 1)
        take = (col == (row // capacity) * padded + row % capacity).astype(F32)
        return jnp.dot(take, rows, precision=HIGHEST, preferred_element_type=F32)

    received = jnp.transpose(compact(in_points[...]))[:16]
    flag = received[comps:comps + 1]
    strain = jnp.where(iota((16, columns), 0) < comps, received, 0.0)
    hard = basis_cols[:, 48:49] * flag

    arrive(gram_copies)
    ghost_basis = jnp.concatenate([
        jnp.concatenate([prev_map, next_map], axis=1),
        jnp.concatenate([prev_image, next_image], axis=1),
        jnp.concatenate(
            [gram_buf[behind, 16:32][:, block:], gram_buf[after, 16:32][:, :block]], axis=1
        ),
        jnp.concatenate([prev_edge[32:48, block:], next_edge[32:48, :block]], axis=1),
    ], axis=0)
    ghost_cols = jnp.transpose(ghost_basis)
    ghost_hard = ghost_cols[:, 48:49] * flag
    gram = gathered(gram_buf)
    forms = jnp.concatenate(
        [gram[0:16, 0:16], gram[0:16, 16:32], gram[0:16, 32:48], gram[0:16, 48:64]], axis=0
    )
    forms = jnp.dot(forms, strain, precision=HIGHEST, preferred_element_type=F32)
    norm = col_sum(forms[0:16] * strain)
    curve = col_sum(forms[16:32] * strain)
    third = col_sum(forms[32:48] * strain)
    fourth = col_sum(forms[48:64] * strain)

    def second_step(norm, curve, left_norm, left_curve, cross):
        ratio = left_norm / (norm + EPSILON)
        next_curve = left_curve + ratio * (2.0 * cross + ratio * curve)
        next_curve = jnp.maximum(next_curve, 0.09 * left_norm)
        next_len = left_norm / (next_curve + EPSILON)
        return next_len, next_len * ratio

    step_len = norm / (curve + EPSILON)
    left_norm = jnp.maximum(norm - step_len * (2.0 * curve - step_len * third), 0.0)
    left_curve = curve - step_len * (2.0 * third - step_len * fourth)
    cross = curve - step_len * third
    next_len, carried = second_step(norm, curve, left_norm, left_curve, cross)
    along = step_len + carried + next_len
    across = next_len * step_len
    zero = jnp.zeros_like(strain)
    weights = jnp.concatenate([
        jnp.concatenate([along * strain, -across * strain, zero], axis=0),
        jnp.concatenate([strain, -along * strain, across * strain], axis=0),
    ], axis=1)
    both = jnp.dot(
        jnp.concatenate([basis_cols[:, :48], ghost_cols[:, :48]], axis=0), weights,
        precision=HIGHEST, preferred_element_type=F32,
    )
    solved = both[:dofs, :columns]
    hard_square = hard * solved * solved
    tangent = 3.0 * hard_square
    residue = both[:dofs, columns:] - hard_square * solved
    ghost_solved = both[dofs:, :columns]
    ghost = both[dofs:, columns:] - ghost_hard * ghost_solved * ghost_solved * ghost_solved

    def coupled(product, ghost):
        top = product[:block] - apply_split(own_high, own_low, ghost[:block])
        bottom = product[dofs - block:] - apply_split(next_high, next_low, ghost[block:])
        return jnp.concatenate([top, product[block:dofs - block], bottom], axis=0)

    def averaged(values):
        return apply_split(average_high, average_low, values)[:comps]

    image = coupled(apply_split(stiff_high[...], stiff_low[...], residue), ghost)
    image = image + tangent * residue
    first_buf[part] = pad_rows(jnp.concatenate([
        col_sum(residue * residue), col_sum(residue * image),
    ], axis=0), first_buf.shape[1])
    first_copies = share(first_buf, first_send, first_recv)
    halo_out[0] = image[:block]
    halo_out[1] = image[dofs - block:]
    halo_copies = to_neighbours(
        halo_out.at[0], halo_out.at[1], halo_in, halo_send, halo_recv
    )
    second = apply_split(stiff_high[...], stiff_low[...], image)
    mean_buf[part] = pad_rows(jnp.concatenate(
        [averaged(solved), averaged(residue), averaged(image)], axis=0
    ), mean_buf.shape[1])
    mean_copies = share(mean_buf, mean_send, mean_recv)
    sends += halo_copies + first_copies + mean_copies
    arrive(first_copies)
    sums = gathered(first_buf)
    norm, curve = sums[0:1], sums[1:2]
    step_len = norm / (curve + EPSILON)
    left = residue - step_len * image
    arrive(halo_copies)
    second = coupled(second, halo_in[...].reshape(2 * block, columns)) + tangent * image
    left_image = image - step_len * second
    second_buf[part] = pad_rows(jnp.concatenate(
        [col_sum(left * left), col_sum(left * left_image), col_sum(left * image)], axis=0
    ), 8)
    second_copies = share(second_buf, second_send, second_recv)
    sends += second_copies
    arrive(mean_copies)
    means = gathered(mean_buf)
    arrive(second_copies)
    last = gathered(second_buf)
    next_len, carried = second_step(norm, curve, last[0:1], last[1:2], last[2:3])
    along = step_len + carried
    total = (
        means[:comps] + along * means[comps:2 * comps]
        + next_len * (means[comps:2 * comps] - step_len * means[2 * comps:3 * comps])
    )

    rows = jnp.transpose(pad_rows(total, LANES))
    if padded != capacity:
        row, col = iota((places, columns), 0), iota((places, columns), 1)
        spread = jnp.logical_and(
            col == (row // padded) * capacity + row % padded, row % padded < capacity
        ).astype(F32)
        rows = jnp.dot(spread, rows, precision=HIGHEST, preferred_element_type=F32)
    out_rows[...] = rows.reshape(groups, padded, LANES)
    row_copies = exchange(out_rows, in_rows, row_send, row_recv)
    sends += row_copies
    in_rows[group] = out_rows[group]
    field_buf[0] = solved + along * residue + next_len * left
    field_copy = pltpu.make_async_copy(field_buf, field_ref, output_sem)
    field_copy.start()
    arrive(row_copies)
    back = jnp.transpose(in_rows[...].reshape(places, LANES))[:16]
    picked = jnp.dot(back, select, precision=HIGHEST, preferred_element_type=F32)
    stress_ref[...] = picked[:comps]
    for copy in sends:
        copy.wait_send()
    field_copy.wait()


def solution(mesh):
    groups, parts = mesh.shape["macro"], mesh.shape["rve"]

    def shards(deform, plastic, route, stiff, cubic, coupling, conn, iface, load_map, average_map):
        comps, points = deform.shape
        blocks, block = coupling.shape[1], coupling.shape[3]
        dofs = blocks * block
        capacity = 2 * points // groups
        columns = groups * capacity
        padded = -(-capacity // 8) * 8
        edge_rows = -(-(2 * comps + 1) // 8) * 8
        vmem = pl.BlockSpec(memory_space=pltpu.VMEM)
        hbm = pl.BlockSpec(memory_space=pltpu.HBM)
        dma = pltpu.SemaphoreType.DMA
        return pl.pallas_call(
            functools.partial(kernel, groups, parts, capacity),
            out_shape=(
                jax.ShapeDtypeStruct((comps, points), F32),
                jax.ShapeDtypeStruct((1, dofs, columns), F32),
            ),
            in_specs=[hbm] * 6 + [pl.BlockSpec(memory_space=pltpu.SMEM)] + [hbm] * 3,
            out_specs=(vmem, hbm),
            scratch_shapes=[
                pltpu.VMEM(deform.shape, F32),
                pltpu.VMEM((1, points), jnp.int32),
                pltpu.VMEM((1, points), jnp.int32),
                pltpu.VMEM((1, dofs), F32),
                pltpu.VMEM((1, dofs), F32),
                pltpu.VMEM(coupling.shape, F32),
                pltpu.VMEM(iface.shape, F32),
                pltpu.VMEM((comps, 1, dofs), F32),
                pltpu.VMEM((comps, 1, dofs), F32),
                pltpu.VMEM((dofs, dofs), F32),
                pltpu.VMEM((dofs, dofs), BF16),
                pltpu.VMEM((dofs, dofs), BF16),
                pltpu.VMEM((groups, padded, LANES), F32),
                pltpu.VMEM((groups, padded, LANES), F32),
                pltpu.VMEM((edge_rows + block // 2, LANES), F32),
                pltpu.VMEM((2, edge_rows + block // 2, LANES), F32),
                pltpu.VMEM((2, block, columns), F32),
                pltpu.VMEM((2, block, columns), F32),
                pltpu.VMEM((parts, 32, LANES), F32),
                pltpu.VMEM((parts, 8, columns), F32),
                pltpu.VMEM((parts, 32, columns), F32),
                pltpu.VMEM((parts, 8, columns), F32),
                pltpu.VMEM((groups, padded, LANES), F32),
                pltpu.VMEM((groups, padded, LANES), F32),
                pltpu.VMEM((1, dofs, columns), F32),
                dma((9,)), dma,
                dma((groups - 1,)), dma((groups - 1,)),
                dma((2,)), dma((2,)),
                dma((2,)), dma((2,)),
                dma((parts - 1,)), dma((parts - 1,)),
                dma((parts - 1,)), dma((parts - 1,)),
                dma((parts - 1,)), dma((parts - 1,)),
                dma((parts - 1,)), dma((parts - 1,)),
                dma((groups - 1,)), dma((groups - 1,)),
            ],
            compiler_params=pltpu.CompilerParams(
                collective_id=0, has_side_effects=True, vmem_limit_bytes=60 * 1024 * 1024
            ),
        )(
            deform, plastic[None], route[None], stiff, cubic, coupling,
            jnp.transpose(conn, (0, 2, 1)), iface,
            jnp.transpose(load_map, (1, 0, 2)), jnp.transpose(average_map, (1, 0, 2)),
        )

    return jax.shard_map(
        shards,
        mesh=mesh,
        in_specs=(
            P(None, "macro"),
            P("macro"),
            P("macro"),
            P("macro", "rve"),
            P("macro", "rve"),
            P("macro", "rve", None, None, None),
            P("macro", "rve", None),
            P("macro", "rve", None),
            P("macro", None, "rve"),
            P("macro", None, "rve"),
        ),
        out_specs=(P(None, "macro"), P("macro", "rve", None)),
        check_vma=False,
    )
```
